256 devices in a mesh: seq: 8 (over y, core), space: 32 (over z, x).
Axes of the slice: x: 4, y: 4, z: 8, core: 2. Of those that a mesh axis runs over, the one named last changes fastest.
Arguments:
- features: bfloat16 [2048, 65536], P(None, ('seq', 'space')), may hold values from -6 to 6
- targets: bfloat16 [2048, 65536], P(None, ('seq', 'space')), may hold values from -6 to 6
- write_keys: bfloat16 [128, 65536], P(None, ('seq', 'space')), may hold values from -0.5 to 0.5
- read_queries: bfloat16 [128, 65536], P(None, ('seq', 'space')), may hold values from -0.0234375 to 0.0234375
- decay_codes: int32 [32, 65536], P('space', 'seq'), may hold values from 0 to 99, as said below
- scan_order: int32 [8192], replicated, may hold values from 0 to 8191, each once
- masked: int32 [49152], P(('seq', 'space')), may hold values from 0 to 65535, as said below
- skip_gain: float32 [32], P('space'), may hold values from 0.5 to 1.5
Outputs:
- mixed: bfloat16 [2048, 65536], P(None, ('seq', 'space'))
- grad_features: bfloat16 [2048, 65536], P(None, ('seq', 'space'))
The draws below stay inside these ranges and needn't reach their ends.
Inputs may be any that keep to these rules, and one draw needn't show every extreme that they name: `decay_codes`: a token's decay factor for its head is exp(-(0.065536 / 65536) code). `masked`: entries k * 192 to (k + 1) * 192 - 1 are distinct indices among tokens k * 256 to (k + 1) * 256 - 1.
All inputs are finite; a program needn't handle non-finite values.
Results may differ from the reference program's by a relative error of at most 0.0034.
Values may be sent and summed in bfloat16 or wider, within the bound.
No kernel may reach another device: no remote copies, remote signals or barrier semaphores. Data moves between devices by JAX's collectives and lax.ppermute only.
A program may use at most 128 MiB of HBM per device.

```python
import jax
import jax.numpy as jnp
from jax import lax

HEAD_TOTAL = 32
STATE = 128
TOK_DEV = 256
INNER = 2048
TOK_SEQ = 8192
CLIP_TOKENS = 65536
MASK_DEV = 192


def draw_decay_codes(key, part):
    random_key_speed, random_key_base, random_key_spike, random_key_bigger = jax.random.split(key, 4)
    group_count = CLIP_TOKENS // TOK_SEQ
    ceiling_table = jnp.array([2, 4, 8, 16, 32, 64, 99], jnp.int32)
    ceiling_pick = jax.random.randint(random_key_speed, (HEAD_TOTAL, group_count, 1), 0, 7)
    ceiling = jnp.take(ceiling_table, ceiling_pick)
    shared_default = jax.random.randint(random_key_base, (HEAD_TOTAL, group_count, TOK_SEQ), 0, ceiling)
    shared_default = shared_default.reshape(HEAD_TOTAL, CLIP_TOKENS)
    sudden_spike = jax.random.randint(random_key_spike, (HEAD_TOTAL, CLIP_TOKENS), 0, 256)
    bigger_variant = jax.random.randint(random_key_bigger, (HEAD_TOTAL, CLIP_TOKENS), 80, 100)
    return jnp.where(sudden_spike == 0, bigger_variant, shared_default).astype(jnp.int32)


def draw_masked(key, part):
    groups = CLIP_TOKENS // TOK_DEV
    keys = jax.random.split(key, groups)
    picks = jax.vmap(lambda sub_key: jax.random.permutation(sub_key, TOK_DEV)[:MASK_DEV])(keys)
    offsets = jnp.arange(groups, dtype=jnp.int32)[:, None] * TOK_DEV
    return (picks.astype(jnp.int32) + offsets).reshape(-1).astype(jnp.int32)


def shard_levels(own_key, extent, cuts, low, top_value):
    factor_of = 1.0
    for dim, parts in cuts:
        draws = jax.random.uniform(jax.random.fold_in(jax.random.fold_in(own_key, 6), dim), (parts,), jnp.float32, low / len(cuts), top_value / len(cuts))
        factor_of = factor_of * jnp.repeat(jnp.exp(draws), extent[dim] // parts).reshape((-1,) + (1,) * (len(extent) - 1 - dim))
    return factor_of


def gaussian(key, extent, scale, limit, cuts=(), held_as=jnp.bfloat16):
    values = scale * jax.random.normal(key, extent, jnp.float32)
    if cuts:
        values = values * shard_levels(key, extent, cuts, -0.22, 0.18)
    return jnp.clip(values, -limit, limit).astype(held_as)


def setup_inputs(seed: int = 0) -> dict:
    arg_keys = jax.random.split(jax.random.key(seed), 9)
    features = gaussian(arg_keys[0], (INNER, CLIP_TOKENS), 1.0, 6.0, ((1, 256),))
    targets = gaussian(arg_keys[1], (INNER, CLIP_TOKENS), 1.0, 6.0, ((1, 256),))
    write_keys = gaussian(arg_keys[2], (STATE, CLIP_TOKENS), STATE ** -0.5, 0.5, ((1, 256),))
    read_queries = gaussian(arg_keys[3], (STATE, CLIP_TOKENS), CLIP_TOKENS ** -0.5, 0.0234375, ((1, 256),))
    decay_codes = draw_decay_codes(jax.random.fold_in(arg_keys[8], 71), 0)
    scan_order = jax.random.permutation(arg_keys[5], TOK_SEQ).astype(jnp.int32)
    masked = draw_masked(jax.random.fold_in(arg_keys[8], 71), 0)
    skip_gain = jnp.clip(0.5 + 1.0 * jax.random.uniform(arg_keys[7], (HEAD_TOTAL,), jnp.float32) ** shard_levels(arg_keys[7], (HEAD_TOTAL,), ((0, 32),), -0.2, 0.2), 0.5, 1.5)
    return {"features": features, "targets": targets, "write_keys": write_keys, "read_queries": read_queries, "decay_codes": decay_codes, "scan_order": scan_order, "masked": masked, "skip_gain": skip_gain}


highest = lax.Precision.HIGHEST


def fading(amount):
    return jnp.exp(-(0.065536 / CLIP_TOKENS) * amount.astype(jnp.float32))


def mix_head(values, into_state, from_state, running, block_size):
    head_width, length = values.shape
    state_count = into_state.shape[0]
    block_count = length // block_size
    value_blocks = values.reshape(head_width, block_count, block_size).transpose(1, 0, 2)
    into_blocks = into_state.reshape(state_count, block_count, block_size).transpose(1, 0, 2)
    from_blocks = from_state.reshape(state_count, block_count, block_size).transpose(1, 0, 2)
    step_blocks = running.reshape(block_count, block_size)
    starting = jnp.concatenate([jnp.zeros((1,), jnp.int32), step_blocks[:-1, -1].astype(jnp.int32)])
    zero_state = jnp.zeros((state_count, head_width), jnp.float32)

    def forward_blocks(state_sum, pieces):
        value_block, into_block, from_block, step_block, earlier = pieces
        latest = step_block[-1]
        gram_block = jnp.dot(into_block.T, from_block, precision=highest)
        weights = (gram_block * fading(jnp.abs(step_block[None, :] - step_block[:, None]))).astype(jnp.bfloat16)
        inside = jnp.dot(value_block.astype(jnp.bfloat16), weights, preferred_element_type=jnp.float32).astype(jnp.float32)
        readout = jnp.dot(state_sum.T, from_block * fading(step_block - earlier)[None, :], precision=highest)
        update = jnp.dot(into_block * fading(latest - step_block)[None, :], value_block.T, precision=highest)
        return state_sum * fading(latest - earlier) + update, inside + readout

    def reverse_blocks(state_sum, pieces):
        value_block, into_block, from_block, step_block, earlier = pieces
        latest = step_block[-1]
        readout = jnp.dot(state_sum.T, from_block * fading(latest - step_block)[None, :], precision=highest)
        update = jnp.dot(into_block * fading(step_block - earlier)[None, :], value_block.T, precision=highest)
        return state_sum * fading(latest - earlier) + update, readout

    sequence = (value_blocks, into_blocks, from_blocks, step_blocks, starting)
    forward_out = lax.scan(forward_blocks, zero_state, sequence)[1]
    reverse_out = lax.scan(reverse_blocks, zero_state, sequence, reverse=True)[1]
    return (forward_out + reverse_out).transpose(1, 0, 2).reshape(head_width, length)


def reference(features, targets, write_keys, read_queries, decay_codes, scan_order, masked, skip_gain):
    inner, tokens = features.shape
    head_count = decay_codes.shape[0]
    head_width = inner // head_count
    seq_share = scan_order.shape[0]
    position = (jnp.arange(tokens // seq_share, dtype=jnp.int32)[:, None] * seq_share + scan_order[None, :].astype(jnp.int32)).reshape(-1).astype(jnp.int32)
    undo = jnp.zeros((tokens,), jnp.int32).at[position].set(jnp.arange(tokens, dtype=jnp.int32))
    block_size = min(512, seq_share)
    into_state = write_keys.astype(jnp.float32)[:, position]
    from_state = read_queries.astype(jnp.float32)[:, position]
    running = jnp.cumsum(decay_codes[:, position], axis=1).astype(jnp.int32)
    per_head = features.reshape(head_count, head_width, tokens)

    def forward_head(triple):
        values = triple[0].astype(jnp.float32)[:, position]
        return mix_head(values, into_state, from_state, triple[1], block_size) + triple[2] * values

    mixed_scan = lax.map(forward_head, (per_head, running, skip_gain))
    mixed = mixed_scan.reshape(inner, tokens)[:, undo].astype(jnp.bfloat16)
    mask_row = jnp.zeros((tokens,), jnp.float32).at[masked].set(1.0)
    residue = (mask_row[None, :] * (mixed.astype(jnp.float32) - targets.astype(jnp.float32))).astype(jnp.bfloat16)
    residue_heads = residue.reshape(head_count, head_width, tokens)

    def backward_head(triple):
        values = triple[0].astype(jnp.float32)[:, position]
        return mix_head(values, from_state, into_state, triple[1], block_size) + triple[2] * values

    grads_scan = lax.map(backward_head, (residue_heads, running, skip_gain))
    grad_features = grads_scan.reshape(inner, tokens)[:, undo].astype(jnp.bfloat16)
    return mixed, grad_features
```

```python
from functools import partial

import jax
import jax.numpy as jnp
from jax import lax
from jax.experimental import pallas as pl
from jax.experimental.pallas import tpu as pltpu
from jax.sharding import PartitionSpec as P

BLOCK = 512
ROWS = 16
f32, bf16 = jnp.float32, jnp.bfloat16
vmem = pl.BlockSpec(memory_space=pltpu.VMEM)
smem = pl.BlockSpec(memory_space=pltpu.SMEM)


def call(kernel, outs, ins, scratch, limit, flops, name):
    specs = [smem if s else vmem for _, s in ins]
    args = [a for a, _ in ins]
    moved = sum(a.size * a.dtype.itemsize for a in args)
    moved += sum(o.size * o.dtype.itemsize for o in outs)
    return pl.pallas_call(
        kernel,
        out_shape=outs,
        in_specs=specs,
        out_specs=[vmem] * len(outs),
        scratch_shapes=scratch,
        compiler_params=pltpu.CompilerParams(vmem_limit_bytes=limit << 20),
        cost_estimate=pl.CostEstimate(flops=flops, bytes_accessed=moved, transcendentals=0),
        name=name,
    )(*args)


def struct(shape, dtype):
    return jax.ShapeDtypeStruct(shape, dtype)


def left_half(shape):
    return lax.broadcasted_iota(jnp.int32, shape, 1) < shape[1] // 2


def split(value):
    high = value.astype(bf16)
    return high, (value - high.astype(f32)).astype(bf16)


def gather_rows(order, first, pairs):
    count = pairs[0][1].shape[0] * 8

    def some(j, _):
        for i in range(ROWS):
            row = order[first + j * ROWS + i]
            for src, dst in pairs:
                dst[j * (ROWS // 8) + i // 8, pl.ds(i % 8, 1), :] = src[pl.ds(row, 1), :]
        return 0

    lax.fori_loop(0, count // ROWS, some, 0)


def scatter_rows(order, first, src, dst):
    count = src.shape[0] * 8

    def some(j, _):
        for i in range(ROWS):
            row = order[first + j * ROWS + i]
            dst[pl.ds(row, 1), :] = src[j * (ROWS // 8) + i // 8, pl.ds(i % 8, 1), :]
        return 0

    lax.fori_loop(0, count // ROWS, some, 0)


def sides_kernel(order, gathered, q_out, w_out, qt_out, wt_out, mask_out, q_all, w_all, q_blk, w_blk):
    chunks, blocks = gathered.shape[0], q_out.shape[0]
    tok = (gathered.shape[1] - 16) // 2

    def unpack(c, _):
        base = pl.multiple_of(c * tok, tok)
        w_all[pl.ds(base, tok), :] = gathered[c, 0:tok, :].astype(f32)
        q_all[pl.ds(base, tok), :] = gathered[c, tok : 2 * tok, :].astype(f32)
        mask_out[c] = gathered[c, 2 * tok : 2 * tok + 16, :].astype(f32)[0:8, :]
        return 0

    lax.fori_loop(0, chunks, unpack, 0)

    def block(b, _):
        gather_rows(order, b * BLOCK, [(q_all, q_blk), (w_all, w_blk)])
        q = q_blk[...].reshape(BLOCK, 128)
        w = w_blk[...].reshape(BLOCK, 128)
        q_out[b] = q.astype(bf16)
        w_out[b] = w.astype(bf16)
        qt_out[b] = q.T.astype(bf16)
        wt_out[b] = w.T.astype(bf16)
        return 0

    lax.fori_loop(0, blocks, block, 0)


def states_kernel(unit, residual, order, *refs):
    if residual:
        mixed, targets, mask, codes, into_t, x_out, e_out, p_out, pay_out, x_all, x_blk, tri = refs
    else:
        values, codes, into_t, x_out, e_out, p_out, pay_out, x_all, x_blk, tri = refs
    chunks, width, tok = codes.shape[0], 64, codes.shape[2]
    blocks = x_out.shape[0]

    def load(c, _):
        base = pl.multiple_of(c * tok, tok)
        if residual:
            row = mask[c]
            wide = jnp.concatenate([row[0:1, :], row[1:2, :]], axis=1)
            part = wide * (mixed[c].astype(f32) - targets[c].astype(f32))
            part = part.astype(bf16).astype(f32)
        else:
            part = values[c].astype(f32)
        code = jnp.broadcast_to(codes[c], (width, tok))
        x_all[pl.ds(base, tok), :] = jnp.concatenate([part, code], axis=0).T
        return 0

    lax.fori_loop(0, chunks, load, 0)
    tri[...] = jnp.where(
        lax.broadcasted_iota(jnp.int32, (BLOCK, BLOCK), 0)
        >= lax.broadcasted_iota(jnp.int32, (BLOCK, BLOCK), 1),
        1.0,
        0.0,
    ).astype(bf16)
    total = jnp.sum(codes[...])
    left = left_half((BLOCK, 128))
    rate = jnp.where(left, unit, -unit)

    def block(b, state):
        earlier, summed = state
        gather_rows(order, b * BLOCK, [(x_all, x_blk)])
        x = x_blk[...].reshape(BLOCK, 128)
        reach = jnp.dot(tri[...], x.astype(bf16), preferred_element_type=f32) + earlier
        wide = jnp.where(left, pltpu.roll(reach, 64, 1), reach)
        e = jnp.exp(rate * (wide - 0.5 * total))
        both = jnp.where(left, x, pltpu.roll(x, 64, 1))
        high, low = split(both * e)
        p = jnp.dot(
            into_t[b], jnp.concatenate([high, low], axis=1), preferred_element_type=f32
        )
        p = p[:, :128] + p[:, 128:]
        x_out[b] = both.astype(bf16)
        e_out[b] = e
        p_out[b] = p
        return reach[BLOCK - 1 : BLOCK, :], summed + p

    zero = (jnp.zeros((1, 128), f32), jnp.zeros((128, 128), f32))
    _, summed = lax.fori_loop(0, blocks, block, zero)
    pay_out[0:128, :] = summed
    pay_out[128:136, :] = jnp.full((8, 128), total, f32)


def inside_kernel(from_ref, into_t, x_ref, e_ref, out):
    lower = lax.broadcasted_iota(jnp.int32, (BLOCK, BLOCK), 0) >= lax.broadcasted_iota(
        jnp.int32, (BLOCK, BLOCK), 1
    )

    def block(b, _):
        gram = jnp.dot(from_ref[b], into_t[b], preferred_element_type=f32)
        gram = jnp.where(lower, gram, 0.0).astype(bf16)
        scaled = (x_ref[b].astype(f32) * e_ref[b]).astype(bf16)
        out[b] = jnp.dot(gram, scaled, preferred_element_type=f32)
        return 0

    lax.fori_loop(0, out.shape[0], block, 0)


def finish_kernel(unit, order, where, skip, from_ref, x_ref, e_ref, in_ref, p_ref, others, out, fr, y_blk, y_all):
    blocks, chunks, tok = x_ref.shape[0], out.shape[0], out.shape[2]
    groups = others.shape[0]
    me = where[0]
    gain = skip[0]
    half = left_half((1, 128))
    centers = []
    before = jnp.zeros((1, 128), f32)
    for g in range(groups):
        size = others[g, 128:129, :]
        centers.append(before + 0.5 * size)
        before = before + size
    mine = jnp.zeros((1, 128), f32)
    for g in range(groups):
        mine = mine + jnp.where(me == g, centers[g], 0.0)
    init = jnp.zeros((128, 128), f32)
    for g in range(groups):
        factor = jnp.exp(-unit * jnp.abs(mine - centers[g]))
        ahead = jnp.where(g < me, factor, 0.0)
        behind = jnp.where(g > me, factor, 0.0)
        init = init + others[g, 0:128, :] * jnp.where(half, ahead, behind)
    left = left_half((128, 128))

    def forward(b, run):
        fr[b, :, 0:128] = run
        return run + p_ref[b]

    lax.fori_loop(0, blocks, forward, init)

    def backward(i, run):
        b = blocks - 1 - i
        run = run + p_ref[b]
        high, low = split(jnp.where(left, fr[b, :, 0:128], run))
        fr[b, :, 0:128] = high.astype(f32)
        fr[b, :, 128:256] = low.astype(f32)
        return run

    lax.fori_loop(0, blocks, backward, init)
    wide = left_half((BLOCK, 128))

    def block(b, _):
        read = jnp.dot(from_ref[b], fr[b].astype(bf16), preferred_element_type=f32)
        near = in_ref[b]
        z = read[:, :128] + read[:, 128:] + jnp.where(wide, near, -near)
        z = z * pltpu.roll(e_ref[b], 64, 1)
        y = z + pltpu.roll(z, 64, 1) + gain * x_ref[b].astype(f32)
        y_blk[...] = y.reshape(BLOCK // 8, 8, 128)
        scatter_rows(order, b * BLOCK, y_blk, y_all)
        return 0

    lax.fori_loop(0, blocks, block, 0)

    def store(c, _):
        base = pl.multiple_of(c * tok, tok)
        out[c] = y_all[pl.ds(base, tok), :].T[0:64, :].astype(bf16)
        return 0

    lax.fori_loop(0, chunks, store, 0)


def per_device(
    features, targets, write_keys, read_queries, decay_codes, scan_order, masked, skip_gain
):
    space_size = lax.axis_size("space")
    seq_size = lax.axis_size("seq")
    state = write_keys.shape[0]
    tok = features.shape[1]
    length = tok * space_size
    blocks = length // BLOCK
    unit = 0.065536 / (length * seq_size)
    width = features.shape[0] // space_size
    seq_place = lax.axis_index("seq")
    first_token = (seq_place * space_size + lax.axis_index("space")) * tok

    def swap(a, axis):
        return lax.all_to_all(a, axis, split_axis=0, concat_axis=0, tiled=True)

    head_x = swap(features.reshape(space_size, width, tok), "space")
    slot_grid = lax.broadcasted_iota(jnp.int32, (masked.shape[0], tok), 1)
    mask_row = jnp.max(
        jnp.where((masked - first_token)[:, None] == slot_grid, 1.0, 0.0), axis=0
    ).astype(bf16)
    packet = jnp.concatenate(
        [
            write_keys.T,
            read_queries.T,
            mask_row.reshape(tok // state, state),
            jnp.zeros((16 - tok // state, state), bf16),
        ],
        axis=0,
    )
    gathered = lax.all_gather(packet, "space", axis=0, tiled=False)
    head_targets = swap(targets.reshape(space_size, width, tok), "space")
    codes = decay_codes.astype(f32).reshape(space_size, 1, tok)
    where = seq_place.reshape(1).astype(jnp.int32)

    by_block = struct((blocks, BLOCK, state), bf16)
    by_block_t = struct((blocks, state, BLOCK), bf16)
    wide = struct((blocks, BLOCK, 128), f32)
    small = pltpu.VMEM((BLOCK // 8, 8, 128), f32)
    full = pltpu.VMEM((length, 128), f32)
    q, w, q_t, w_t, mask = call(
        sides_kernel,
        [by_block, by_block, by_block_t, by_block_t, struct((space_size, 8, 128), f32)],
        [(scan_order, True), (gathered, False)],
        [full, full, small, small],
        40,
        10**9,
        "sides",
    )

    def mixing(sources, residual, into_t, from_side):
        x, e, p, pay = call(
            partial(states_kernel, unit, residual),
            [by_block, wide, struct((blocks, state, 128), f32), struct((state + 8, 128), f32)],
            [(scan_order, True), *sources, (codes, False), (into_t, False)],
            [full, small, pltpu.VMEM((BLOCK, BLOCK), bf16)],
            40,
            2 * 10**9,
            "states",
        )
        others = swap(jnp.broadcast_to(pay[None], (seq_size,) + pay.shape), "seq")
        near = call(
            inside_kernel,
            [wide],
            [(from_side, False), (into_t, False), (x, False), (e, False)],
            [],
            40,
            4 * 10**9,
            "inside",
        )[0]
        return call(
            partial(finish_kernel, unit),
            [struct((space_size, width, tok), bf16)],
            [
                (scan_order, True),
                (where, True),
                (skip_gain, True),
                (from_side, False),
                (x, False),
                (e, False),
                (near, False),
                (p, False),
                (others, False),
            ],
            [pltpu.VMEM((blocks, state, 256), f32), small, full],
            40,
            2 * 10**9,
            "finish",
        )[0]

    mixed_heads = mixing([(head_x, False)], False, w_t, q)
    mixed = swap(mixed_heads, "space").reshape(features.shape)
    sources = [(mixed_heads, False), (head_targets, False), (mask, False)]
    grads_heads = mixing(sources, True, q_t, w)
    grad_features = swap(grads_heads, "space").reshape(features.shape)
    return (mixed, grad_features)


def solution(mesh):
    return jax.shard_map(
        per_device,
        mesh=mesh,
        in_specs=(
            P(None, ("seq", "space")),
            P(None, ("seq", "space")),
            P(None, ("seq", "space")),
            P(None, ("seq", "space")),
            P("space", "seq"),
            P(),
            P(("seq", "space")),
            P("space"),
        ),
        out_specs=(P(None, ("seq", "space")), P(None, ("seq", "space"))),
        check_vma=False,
    )
```

```python
from functools import partial

import jax
import jax.numpy as jnp
from jax import lax
from jax.experimental import pallas as pl
from jax.experimental.pallas import tpu as pltpu
from jax.sharding import PartitionSpec as P

BLOCK = 512
MARK = 16384.0
f32, bf16 = jnp.float32, jnp.bfloat16
anywhere = pl.BlockSpec(memory_space=pl.ANY)
smem = pl.BlockSpec(memory_space=pltpu.SMEM)


def call(kernel, outs, scalars, arrays, scratch, flops, name):
    args = [*scalars, *arrays]
    moved = sum(a.size * a.dtype.itemsize for a in args)
    moved += sum(o.size * o.dtype.itemsize for o in outs)
    held = [pltpu.VMEM(v.shape, v.dtype) for v in [*arrays, *outs]]
    most = max(v.shape[0] for v in [*arrays, *outs])
    sems = pltpu.SemaphoreType.DMA((len(held), most))
    return pl.pallas_call(
        partial(streaming, kernel, len(scalars), len(arrays), len(outs)),
        out_shape=outs,
        in_specs=[smem] * len(scalars) + [anywhere] * len(arrays),
        out_specs=[anywhere] * len(outs),
        scratch_shapes=[*held, sems, *scratch],
        cost_estimate=pl.CostEstimate(flops=flops, bytes_accessed=moved, transcendentals=0),
        name=name,
    )(*args)


class Stream:
    def __init__(self, far, near, sems):
        self.far, self.near, self.sems = far, near, sems
        self.count, self.shape = near.shape[0], near.shape

    def each(self, act):
        lax.fori_loop(0, self.count, lambda i, _: (act(i), 0)[1], 0)

    def inward(self, i):
        return pltpu.make_async_copy(self.far.at[i], self.near.at[i], self.sems.at[i])

    def outward(self, i):
        return pltpu.make_async_copy(self.near.at[i], self.far.at[i], self.sems.at[i])

    def __getitem__(self, i):
        return self.near[i]

    def take(self, i):
        self.inward(i).wait()
        return self.near[i]

    def give(self, i, value):
        self.near[i] = value
        self.outward(i).start()


def streaming(kernel, n_scalars, n_in, n_out, *refs):
    scalars, refs = refs[:n_scalars], refs[n_scalars:]
    far, refs = refs[: n_in + n_out], refs[n_in + n_out :]
    near, sems, scratch = refs[: n_in + n_out], refs[n_in + n_out], refs[n_in + n_out + 1 :]
    streams = [Stream(f, n, sems.at[k]) for k, (f, n) in enumerate(zip(far, near))]
    for stream in streams[:n_in]:
        stream.each(lambda i, s=stream: s.inward(i).start())
    kernel(*scalars, *streams, *scratch)
    for stream in streams[n_in:]:
        stream.each(lambda i, s=stream: s.outward(i).wait())


def struct(shape, dtype):
    return jax.ShapeDtypeStruct(shape, dtype)


def left_half(shape):
    return lax.broadcasted_iota(jnp.int32, shape, 1) < shape[1] // 2


def lower_part(shape):
    return lax.broadcasted_iota(jnp.int32, shape, 0) >= lax.broadcasted_iota(jnp.int32, shape, 1)


def split(value):
    high = value.astype(bf16)
    return high, (value - high.astype(f32)).astype(bf16)


def gather_rows(order, b, src, dst):
    first = b * BLOCK
    for i in range(BLOCK):
        dst[i // 8, pl.ds(i % 8, 1), :] = src[pl.ds(order[first + i], 1), :]


def scatter_rows(order, b, src, dst):
    first = b * BLOCK
    for i in range(BLOCK):
        dst[pl.ds(order[first + i], 1), :] = src[i // 8, pl.ds(i % 8, 1), :]


def gathered_blocks(order, count, src, bufs, work, init):
    gather_rows(order, 0, src, bufs[0])

    def pair(i, carry):
        for k in range(2):
            b = 2 * i + k
            block = bufs[k][...].reshape(BLOCK, 128)
            gather_rows(order, jnp.minimum(b + 1, count - 1), src, bufs[1 - k])
            carry = work(b, block, carry)
        return carry

    return lax.fori_loop(0, count // 2, pair, init)


def scattered_blocks(order, count, bufs, dst, work):
    def put(k, value):
        bufs[k][...] = value.reshape(BLOCK // 8, 8, 128)

    put(0, work(0))
    put(1, work(1))
    scatter_rows(order, 0, bufs[0], dst)

    def pair(i, _):
        for k in range(2):
            b = 2 * i + k
            scatter_rows(order, b - 1, bufs[1 - k], dst)
            put(k, work(b))
        return 0

    lax.fori_loop(1, count // 2, pair, 0)
    scatter_rows(order, count - 1, bufs[1], dst)


def packet_kernel(write, read, out):
    for k, side in enumerate((write, read)):
        out.give(k, side.take(0).astype(f32).T.astype(bf16))


def decay_kernel(unit, order, codes, e_out, total_out, code_all, tri, *bufs):
    def load(c, sums):
        row = codes.take(c)
        code_all[pl.ds(pl.multiple_of(c * 128, 128), 128), :] = jnp.broadcast_to(row, (128, 128)).T
        return sums + row

    sums = lax.fori_loop(0, codes.count, load, jnp.zeros((1, 128), f32))
    tri[...] = jnp.where(lower_part((BLOCK, BLOCK)), 1.0, 0.0).astype(bf16)
    total = jnp.sum(sums)
    total_out.give(0, jnp.full((8, 128), total, f32))
    rate = jnp.where(left_half((BLOCK, 128)), unit, -unit)

    def block(b, code, earlier):
        reach = jnp.dot(tri[...], code.astype(bf16), preferred_element_type=f32) + earlier
        e_out.give(b, jnp.exp(rate * (reach - 0.5 * total)))
        return reach[BLOCK - 1 : BLOCK, :]

    gathered_blocks(order, e_out.count, code_all, bufs, block, jnp.zeros((1, 128), f32))


def rows_kernel(order, values, targets, xt_out, xt_all, *bufs):
    tok = values.shape[2]

    def load(c, _):
        base = pl.multiple_of(c * tok, tok)
        both = jnp.concatenate([values.take(c).astype(f32), targets.take(c).astype(f32)], axis=0)
        xt_all[pl.ds(base, tok), :] = both.T
        return 0

    lax.fori_loop(0, values.count, load, 0)

    def block(b, rows, _):
        xt_out.give(b, rows.astype(bf16))
        return 0

    gathered_blocks(order, xt_out.count, xt_all, bufs, block, 0)


def block_states(scaled, into_t):
    p = jnp.dot(into_t, jnp.concatenate(split(scaled), axis=1), preferred_element_type=f32)
    return p[:, :128] + p[:, 128:]


def lower_sum(scaled, from_side, into_t):
    gram = jnp.dot(from_side, into_t, preferred_element_type=f32)
    gram = jnp.where(lower_part((BLOCK, BLOCK)), gram, 0.0).astype(bf16)
    return jnp.dot(gram, scaled.astype(bf16), preferred_element_type=f32)


def unpack(sides, side, rows_all):
    tok = sides.shape[2]

    def load(c, _):
        rows_all[pl.ds(pl.multiple_of(c * tok, tok), tok), :] = sides.take(c)[side].astype(f32)
        return 0

    lax.fori_loop(0, sides.count, load, 0)


def doubled(xt):
    x = xt.astype(f32)
    return jnp.where(left_half((BLOCK, 128)), x, pltpu.roll(x, 64, 1))


def states_kernel(order, write, xt_in, e_in, total, w_out, wt_out, p_out, pay_out, rows_all, *bufs):
    unpack(write, 0, rows_all)

    def block(b, w, summed):
        w_t = w.T.astype(bf16)
        w_out.give(b, w.astype(bf16))
        wt_out.give(b, w_t)
        p = block_states(doubled(xt_in.take(b)) * e_in.take(b), w_t)
        p_out.give(b, p)
        return summed + p

    summed = gathered_blocks(order, p_out.count, rows_all, bufs, block, jnp.zeros((128, 128), f32))
    pay_out.give(0, jnp.concatenate([summed, total.take(0)], axis=0))


def near_kernel(order, read, xt_in, e_in, wt_in, q_out, qt_out, near_out, rows_all, *bufs):
    unpack(read, 1, rows_all)

    def block(b, q, _):
        q_low = q.astype(bf16)
        q_out.give(b, q_low)
        qt_out.give(b, q.T.astype(bf16))
        scaled = doubled(xt_in.take(b)) * e_in.take(b)
        near_out.give(b, lower_sum(scaled, q_low, wt_in.take(b)))
        return 0

    gathered_blocks(order, near_out.count, rows_all, bufs, block, 0)


def prepare(unit, me, p_in, others_in, fr):
    groups, blocks = others_in.count, p_in.count
    others = [others_in.take(g) for g in range(groups)]
    half = left_half((1, 128))
    centers = []
    before = jnp.zeros((1, 128), f32)
    for g in range(groups):
        size = others[g][128:129, :]
        centers.append(before + 0.5 * size)
        before = before + size
    mine = jnp.zeros((1, 128), f32)
    for g in range(groups):
        mine = mine + jnp.where(me == g, centers[g], 0.0)
    init = jnp.zeros((128, 128), f32)
    for g in range(groups):
        factor = jnp.exp(-unit * jnp.abs(mine - centers[g]))
        ahead = jnp.where(g < me, factor, 0.0)
        behind = jnp.where(g > me, factor, 0.0)
        init = init + others[g][0:128, :] * jnp.where(half, ahead, behind)
    left = left_half((128, 128))

    def forward(b, run):
        fr[b, :, 0:128] = run
        return run + p_in.take(b)

    lax.fori_loop(0, blocks, forward, init)

    def backward(i, run):
        b = blocks - 1 - i
        run = run + p_in[b]
        high, low = split(jnp.where(left, fr[b, :, 0:128], run))
        fr[b, :, 0:128] = high.astype(f32)
        fr[b, :, 128:256] = low.astype(f32)
        return run

    lax.fori_loop(0, blocks, backward, init)


def read_out(from_side, fr, near, e):
    read = jnp.dot(from_side, fr.astype(bf16), preferred_element_type=f32)
    z = read[:, :128] + read[:, 128:]
    z = z + jnp.where(left_half((BLOCK, 128)), near, -near)
    z = z * pltpu.roll(e, 64, 1)
    return z + pltpu.roll(z, 64, 1)


def store_positions(y_all, out):
    tok = out.shape[2]

    def store(c, _):
        base = pl.multiple_of(c * tok, tok)
        out.give(c, y_all[pl.ds(base, tok), :].T[0:64, :].astype(bf16))
        return 0

    lax.fori_loop(0, out.count, store, 0)


def turn_kernel(unit, where, skip, from_in, from_t, xt_in, e_in, near_in, p_in, total, others, y_out, res_out, p_out, pay_out, fr):
    prepare(unit, where[0], p_in, others, fr)
    gain = skip[0]
    left = left_half((BLOCK, 128))

    def block(b, summed):
        e = e_in.take(b)
        xt = xt_in.take(b).astype(f32)
        tx = pltpu.roll(xt, 64, 1)
        x = jnp.where(left, xt, tx)
        t = jnp.where(left, tx, xt)
        y = (read_out(from_in.take(b), fr[b], near_in.take(b), e) + gain * x).astype(bf16)
        y_out.give(b, y)
        residue = jnp.where(t < 1024.0, y.astype(f32) - t, 0.0).astype(bf16)
        res_out.give(b, residue)
        p = block_states(residue.astype(f32) * e, from_t.take(b))
        p_out.give(b, p)
        return summed + p

    summed = lax.fori_loop(0, p_in.count, block, jnp.zeros((128, 128), f32))
    pay_out.give(0, jnp.concatenate([summed, total.take(0)], axis=0))


def place_kernel(order, y_in, res_in, e_in, into_in, from_t, out, near_out, y_all, *bufs):
    def block(b):
        scaled = res_in.take(b).astype(f32) * e_in.take(b)
        near_out.give(b, lower_sum(scaled, into_in.take(b), from_t.take(b)))
        return y_in.take(b).astype(f32)

    scattered_blocks(order, near_out.count, bufs, y_all, block)
    store_positions(y_all, out)


def finish_kernel(unit, order, where, skip, into_in, res_in, e_in, near_in, p_in, others, out, fr, y_all, *bufs):
    prepare(unit, where[0], p_in, others, fr)
    gain = skip[0]

    def block(b):
        y = read_out(into_in.take(b), fr[b], near_in.take(b), e_in.take(b))
        return y + gain * res_in.take(b).astype(f32)

    scattered_blocks(order, p_in.count, bufs, y_all, block)
    store_positions(y_all, out)


def per_device(
    features, targets, write_keys, read_queries, decay_codes, scan_order, masked, skip_gain
):
    space_size = lax.axis_size("space")
    seq_size = lax.axis_size("seq")
    state = write_keys.shape[0]
    tok = features.shape[1]
    length = tok * space_size
    blocks = length // BLOCK
    unit = 0.065536 / (length * seq_size)
    width = features.shape[0] // space_size
    seq_place = lax.axis_index("seq")
    first_token = (seq_place * space_size + lax.axis_index("space")) * tok

    def swap(a, axis):
        return lax.all_to_all(a, axis, split_axis=0, concat_axis=0, tiled=True)

    packet = call(
        packet_kernel, [struct((2, tok, state), bf16)], [], [write_keys[None], read_queries[None]], [], 0, "packet"
    )[0]
    gathered = lax.all_gather(packet, "space", axis=0, tiled=False)
    head_x = swap(features.reshape(space_size, width, tok), "space")
    slot_grid = lax.broadcasted_iota(jnp.int32, (masked.shape[0], tok), 1)
    is_masked = jnp.any((masked - first_token)[:, None] == slot_grid, axis=0)
    marked = jnp.where(is_masked[None], targets, jnp.asarray(MARK, bf16))
    head_t = swap(marked.reshape(space_size, width, tok), "space")
    codes = decay_codes.astype(f32).reshape(length // 128, 1, 128)
    where = seq_place.reshape(1).astype(jnp.int32)

    by_block = struct((blocks, BLOCK, state), bf16)
    wide = struct((blocks, BLOCK, 128), f32)
    by_block_t = struct((blocks, state, BLOCK), bf16)
    states = struct((blocks, state, 128), f32)
    payload = struct((1, state + 8, 128), f32)
    heads = struct((space_size, width, tok), bf16)
    small = pltpu.VMEM((BLOCK // 8, 8, 128), f32)
    full = pltpu.VMEM((length, 128), f32)
    read_states = pltpu.VMEM((blocks, state, 256), f32)

    e, total = call(
        partial(decay_kernel, unit),
        [wide, struct((1, 8, 128), f32)],
        [scan_order],
        [codes],
        [full, pltpu.VMEM((BLOCK, BLOCK), bf16), small, small],
        2 * 10**9,
        "decay",
    )
    xt = call(rows_kernel, [by_block], [scan_order], [head_x, head_t], [full, small, small], 10**9, "rows")[0]
    w, w_t, p, pay = call(
        states_kernel,
        [by_block, by_block_t, states, payload],
        [scan_order],
        [gathered, xt, e, total],
        [full, small, small],
        2 * 10**9,
        "states",
    )
    others = swap(jnp.broadcast_to(pay, (seq_size,) + pay.shape[1:]), "seq")
    q, q_t, near = call(
        near_kernel,
        [by_block, by_block_t, wide],
        [scan_order],
        [gathered, xt, e, w_t],
        [full, small, small],
        4 * 10**9,
        "near",
    )
    y, residue, p, pay = call(
        partial(turn_kernel, unit),
        [by_block, by_block, states, payload],
        [where, skip_gain],
        [q, q_t, xt, e, near, p, total, others],
        [read_states],
        2 * 10**9,
        "turn",
    )
    others = swap(jnp.broadcast_to(pay, (seq_size,) + pay.shape[1:]), "seq")
    mixed_heads, near = call(
        place_kernel,
        [heads, wide],
        [scan_order],
        [y, residue, e, w, q_t],
        [full, small, small],
        4 * 10**9,
        "place",
    )
    mixed = swap(mixed_heads, "space").reshape(features.shape)
    grads_heads = call(
        partial(finish_kernel, unit),
        [heads],
        [scan_order, where, skip_gain],
        [w, residue, e, near, p, others],
        [read_states, full, small, small],
        2 * 10**9,
        "finish",
    )[0]
    grad_features = swap(grads_heads, "space").reshape(features.shape)
    return (mixed, grad_features)


def solution(mesh):
    return jax.shard_map(
        per_device,
        mesh=mesh,
        in_specs=(
            P(None, ("seq", "space")),
            P(None, ("seq", "space")),
            P(None, ("seq", "space")),
            P(None, ("seq", "space")),
            P("space", "seq"),
            P(),
            P(("seq", "space")),
            P("space"),
        ),
        out_specs=(P(None, ("seq", "space")), P(None, ("seq", "space"))),
        check_vma=False,
    )
```

```python
from functools import partial

import jax
import jax.numpy as jnp
from jax import lax
from jax.experimental import pallas as pl
from jax.experimental.pallas import tpu as pltpu
from jax.sharding import PartitionSpec as P

BLOCK = 512
MARK = 16384.0
f32, bf16 = jnp.float32, jnp.bfloat16
anywhere = pl.BlockSpec(memory_space=pl.ANY)
smem = pl.BlockSpec(memory_space=pltpu.SMEM)


def call(kernel, outs, scalars, arrays, scratch, flops, name, order=None):
    ordered = order is not None
    args = [*scalars, *([order] if ordered else []), *arrays]
    moved = sum(a.size * a.dtype.itemsize for a in args)
    moved += sum(o.size * o.dtype.itemsize for o in outs)
    held = [pltpu.VMEM(v.shape, v.dtype) for v in [*arrays, *outs]]
    most = max(v.shape[0] for v in [*arrays, *outs])
    sems = pltpu.SemaphoreType.DMA((len(held), most))
    return pl.pallas_call(
        partial(streaming, kernel, len(scalars), ordered, len(arrays), len(outs)),
        out_shape=outs,
        in_specs=[smem] * len(scalars) + [anywhere] * (ordered + len(arrays)),
        out_specs=[anywhere] * len(outs),
        scratch_shapes=[*(order_scratch(order) if ordered else []), *held, sems, *scratch],
        cost_estimate=pl.CostEstimate(flops=flops, bytes_accessed=moved, transcendentals=0),
        name=name,
    )(*args)


class Stream:
    def __init__(self, far, near, sems):
        self.far, self.near, self.sems = far, near, sems
        self.count, self.shape = near.shape[0], near.shape

    def each(self, act):
        lax.fori_loop(0, self.count, lambda i, _: (act(i), 0)[1], 0)

    def inward(self, i):
        return pltpu.make_async_copy(self.far.at[i], self.near.at[i], self.sems.at[i])

    def outward(self, i):
        return pltpu.make_async_copy(self.near.at[i], self.far.at[i], self.sems.at[i])

    def __getitem__(self, i):
        return self.near[i]

    def take(self, i):
        self.inward(i).wait()
        return self.near[i]

    def put(self, i, value):
        self.near[i] = value

    def give(self, i, value):
        self.near[i] = value
        self.outward(i).start()


def order_scratch(order):
    return [pltpu.SMEM(order.shape[1:], jnp.int32)] * 2 + [pltpu.SemaphoreType.DMA((2,))]


class Order:
    def __init__(self, far, near, sems):
        self.far, self.near, self.sems = far, near, sems
        self.last = far.shape[0] - 1

    def copy(self, b, k):
        return pltpu.make_async_copy(self.far.at[jnp.minimum(b, self.last)], self.near[k], self.sems.at[k])

    def row(self, k, i):
        return self.near[k][i // 128, i % 128]


def streaming(kernel, n_scalars, ordered, n_in, n_out, *refs):
    scalars, refs = list(refs[:n_scalars]), refs[n_scalars:]
    n = ordered + n_in + n_out
    far, refs = refs[:n], refs[n:]
    if ordered:
        order = Order(far[0], refs[:2], refs[2])
        far, refs = far[1:], refs[3:]
        order.copy(0, 0).start()
        order.copy(1, 1).start()
        scalars = [order, *scalars]
    n -= ordered
    near, sems, scratch = refs[:n], refs[n], refs[n + 1 :]
    streams = [Stream(f, v, sems.at[k]) for k, (f, v) in enumerate(zip(far, near))]
    for stream in streams[:n_in]:
        stream.each(lambda i, s=stream: s.inward(i).start())
    kernel(*scalars, *streams, *scratch)
    for stream in streams[n_in:]:
        stream.each(lambda i, s=stream: s.outward(i).wait())


def struct(shape, dtype):
    return jax.ShapeDtypeStruct(shape, dtype)


def left_half(shape):
    return lax.broadcasted_iota(jnp.int32, shape, 1) < shape[1] // 2


def lower_part(shape):
    return lax.broadcasted_iota(jnp.int32, shape, 0) >= lax.broadcasted_iota(jnp.int32, shape, 1)


def split(value):
    high = value.astype(bf16)
    return high, (value - high.astype(f32)).astype(bf16)


def gather_rows(order, k, src, dst):
    for i in range(BLOCK):
        dst[i // 8, pl.ds(i % 8, 1), :] = src[pl.ds(order.row(k, i), 1), :]


def scatter_rows(order, k, src, dst):
    for i in range(BLOCK):
        dst[pl.ds(order.row(k, i), 1), :] = src[i // 8, pl.ds(i % 8, 1), :]


def arrive(ins, first):
    for stream in ins:
        for k in range(2):
            stream.inward(first + k).wait()


def leave(outs, first):
    for stream in outs:
        for k in range(2):
            stream.outward(first + k).start()


def gathered_blocks(order, src, bufs, ins, outs, work, init):
    order.copy(0, 0).wait()
    gather_rows(order, 0, src, bufs[0])
    order.copy(2, 0).start()

    def pair(i, carry):
        b = 2 * i
        arrive(ins, b)
        order.copy(b + 1, 1).wait()
        order.copy(b + 2, 0).wait()
        block = bufs[0][...].reshape(BLOCK, 128)
        gather_rows(order, 1, src, bufs[1])
        carry = work(b, block, carry)
        block = bufs[1][...].reshape(BLOCK, 128)
        gather_rows(order, 0, src, bufs[0])
        carry = work(b + 1, block, carry)
        order.copy(b + 3, 1).start()
        order.copy(b + 4, 0).start()
        leave(outs, b)
        return carry

    carry = lax.fori_loop(0, outs[0].count // 2, pair, init)
    order.copy(0, 0).wait()
    order.copy(0, 1).wait()
    return carry


def scattered_blocks(order, bufs, dst, ins, outs, work):
    def put(k, value):
        bufs[k][...] = value.reshape(BLOCK // 8, 8, 128)

    arrive(ins, 0)
    order.copy(0, 0).wait()
    put(0, work(0))
    scatter_rows(order, 0, bufs[0], dst)
    put(1, work(1))
    order.copy(2, 0).start()
    leave(outs, 0)

    def pair(i, _):
        b = 2 * i
        arrive(ins, b)
        order.copy(b - 1, 1).wait()
        order.copy(b, 0).wait()
        scatter_rows(order, 1, bufs[1], dst)
        put(0, work(b))
        scatter_rows(order, 0, bufs[0], dst)
        put(1, work(b + 1))
        order.copy(b + 1, 1).start()
        order.copy(b + 2, 0).start()
        leave(outs, b)
        return 0

    lax.fori_loop(1, ins[0].count // 2, pair, 0)
    order.copy(0, 1).wait()
    scatter_rows(order, 1, bufs[1], dst)
    order.copy(0, 0).wait()


def packet_kernel(write, read, out):
    for k, side in enumerate((write, read)):
        out.give(k, side.take(0).astype(f32).T.astype(bf16))


def decay_kernel(unit, order, codes, e_out, total_out, code_all, tri, *bufs):
    def load(c, sums):
        row = codes.take(c)
        code_all[pl.ds(pl.multiple_of(c * 128, 128), 128), :] = jnp.broadcast_to(row, (128, 128)).T
        return sums + row

    sums = lax.fori_loop(0, codes.count, load, jnp.zeros((1, 128), f32))
    tri[...] = jnp.where(lower_part((BLOCK, BLOCK)), 1.0, 0.0).astype(bf16)
    total = jnp.sum(sums)
    total_out.give(0, jnp.full((8, 128), total, f32))
    rate = jnp.where(left_half((BLOCK, 128)), unit, -unit)

    def block(b, code, earlier):
        reach = jnp.dot(tri[...], code.astype(bf16), preferred_element_type=f32) + earlier
        e_out.put(b, jnp.exp(rate * (reach - 0.5 * total)))
        return reach[BLOCK - 1 : BLOCK, :]

    gathered_blocks(order, code_all, bufs, [], [e_out], block, jnp.zeros((1, 128), f32))


def rows_kernel(order, values, targets, xt_out, xt_all, *bufs):
    tok = values.shape[2]

    def load(c, _):
        base = pl.multiple_of(c * tok, tok)
        both = jnp.concatenate([values.take(c).astype(f32), targets.take(c).astype(f32)], axis=0)
        xt_all[pl.ds(base, tok), :] = both.T
        return 0

    lax.fori_loop(0, values.count, load, 0)

    def block(b, rows, _):
        xt_out.put(b, rows.astype(bf16))
        return 0

    gathered_blocks(order, xt_all, bufs, [], [xt_out], block, 0)


def block_states(scaled, into_t):
    p = jnp.dot(into_t, jnp.concatenate(split(scaled), axis=1), preferred_element_type=f32)
    return p[:, :128] + p[:, 128:]


def lower_sum(scaled, from_side, into_t):
    half = BLOCK // 2
    low = scaled.astype(bf16)
    top = jnp.dot(from_side[:half], into_t[:, :half], preferred_element_type=f32)
    end = jnp.dot(from_side[half:], into_t, preferred_element_type=f32)
    keep = lower_part((half, half))
    top = jnp.where(keep, top, 0.0).astype(bf16)
    end = jnp.concatenate([end[:, :half], jnp.where(keep, end[:, half:], 0.0)], axis=1).astype(bf16)
    top = jnp.dot(top, low[:half], preferred_element_type=f32)
    end = jnp.dot(end, low, preferred_element_type=f32)
    return jnp.concatenate([top, end], axis=0)


def unpack(sides, side, rows_all):
    tok = sides.shape[2]

    def load(c, _):
        rows_all[pl.ds(pl.multiple_of(c * tok, tok), tok), :] = sides.take(c)[side].astype(f32)
        return 0

    lax.fori_loop(0, sides.count, load, 0)


def doubled(xt):
    x = xt.astype(f32)
    return jnp.where(left_half((BLOCK, 128)), x, pltpu.roll(x, 64, 1))


def states_kernel(order, write, xt_in, e_in, total, w_out, wt_out, p_out, pay_out, rows_all, *bufs):
    unpack(write, 0, rows_all)

    def block(b, w, summed):
        w_t = w.T.astype(bf16)
        w_out.put(b, w.astype(bf16))
        wt_out.put(b, w_t)
        p = block_states(doubled(xt_in[b]) * e_in[b], w_t)
        p_out.put(b, p)
        return summed + p

    zero = jnp.zeros((128, 128), f32)
    summed = gathered_blocks(order, rows_all, bufs, [xt_in, e_in], [w_out, wt_out, p_out], block, zero)
    pay_out.give(0, jnp.concatenate([summed, total.take(0)], axis=0))


def near_kernel(order, read, xt_in, e_in, wt_in, q_out, qt_out, near_out, rows_all, *bufs):
    unpack(read, 1, rows_all)

    def block(b, q, _):
        q_low = q.astype(bf16)
        q_out.put(b, q_low)
        qt_out.put(b, q.T.astype(bf16))
        near_out.put(b, lower_sum(doubled(xt_in[b]) * e_in[b], q_low, wt_in[b]))
        return 0

    gathered_blocks(order, rows_all, bufs, [xt_in, e_in, wt_in], [q_out, qt_out, near_out], block, 0)


def prepare(unit, me, p_in, others_in, fr):
    groups, blocks = others_in.count, p_in.count
    others = [others_in.take(g) for g in range(groups)]
    half = left_half((1, 128))
    centers = []
    before = jnp.zeros((1, 128), f32)
    for g in range(groups):
        size = others[g][128:129, :]
        centers.append(before + 0.5 * size)
        before = before + size
    mine = jnp.zeros((1, 128), f32)
    for g in range(groups):
        mine = mine + jnp.where(me == g, centers[g], 0.0)
    init = jnp.zeros((128, 128), f32)
    for g in range(groups):
        factor = jnp.exp(-unit * jnp.abs(mine - centers[g]))
        ahead = jnp.where(g < me, factor, 0.0)
        behind = jnp.where(g > me, factor, 0.0)
        init = init + others[g][0:128, :] * jnp.where(half, ahead, behind)
    left = left_half((128, 128))

    def forward(b, run):
        fr[b, :, 0:128] = run
        return run + p_in.take(b)

    lax.fori_loop(0, blocks, forward, init)

    def backward(i, run):
        b = blocks - 1 - i
        run = run + p_in[b]
        high, low = split(jnp.where(left, fr[b, :, 0:128], run))
        fr[b, :, 0:128] = high.astype(f32)
        fr[b, :, 128:256] = low.astype(f32)
        return run

    lax.fori_loop(0, blocks, backward, init)


def read_out(from_side, fr, near, e):
    read = jnp.dot(from_side, fr.astype(bf16), preferred_element_type=f32)
    z = read[:, :128] + read[:, 128:]
    z = z + jnp.where(left_half((BLOCK, 128)), near, -near)
    z = z * pltpu.roll(e, 64, 1)
    return z + pltpu.roll(z, 64, 1)


def store_positions(y_all, out):
    tok = out.shape[2]

    def store(c, _):
        base = pl.multiple_of(c * tok, tok)
        out.give(c, y_all[pl.ds(base, tok), :].T[0:64, :].astype(bf16))
        return 0

    lax.fori_loop(0, out.count, store, 0)


def turn_kernel(unit, where, skip, from_in, from_t, xt_in, e_in, near_in, p_in, total, others, y_out, res_out, p_out, pay_out, fr):
    prepare(unit, where[0], p_in, others, fr)
    gain = skip[0]
    left = left_half((BLOCK, 128))

    ins = [from_in, from_t, xt_in, e_in, near_in]

    def block(b, summed):
        e = e_in[b]
        xt = xt_in[b].astype(f32)
        tx = pltpu.roll(xt, 64, 1)
        x = jnp.where(left, xt, tx)
        t = jnp.where(left, tx, xt)
        y = (read_out(from_in[b], fr[b], near_in[b], e) + gain * x).astype(bf16)
        y_out.put(b, y)
        residue = jnp.where(t < 1024.0, y.astype(f32) - t, 0.0).astype(bf16)
        res_out.put(b, residue)
        p = block_states(residue.astype(f32) * e, from_t[b])
        p_out.put(b, p)
        return summed + p

    def pair(i, summed):
        arrive(ins, 2 * i)
        summed = block(2 * i + 1, block(2 * i, summed))
        leave([y_out, res_out, p_out], 2 * i)
        return summed

    summed = lax.fori_loop(0, p_in.count // 2, pair, jnp.zeros((128, 128), f32))
    pay_out.give(0, jnp.concatenate([summed, total.take(0)], axis=0))


def place_kernel(order, y_in, res_in, e_in, into_in, from_t, out, near_out, y_all, *bufs):
    def block(b):
        near_out.put(b, lower_sum(res_in[b].astype(f32) * e_in[b], into_in[b], from_t[b]))
        return y_in[b].astype(f32)

    scattered_blocks(order, bufs, y_all, [y_in, res_in, e_in, into_in, from_t], [near_out], block)
    store_positions(y_all, out)


def finish_kernel(unit, order, where, skip, into_in, res_in, e_in, near_in, p_in, others, out, fr, y_all, *bufs):
    prepare(unit, where[0], p_in, others, fr)
    gain = skip[0]

    def block(b):
        y = read_out(into_in[b], fr[b], near_in[b], e_in[b])
        return y + gain * res_in[b].astype(f32)

    scattered_blocks(order, bufs, y_all, [into_in, res_in, e_in, near_in], [], block)
    store_positions(y_all, out)


def per_device(
    features, targets, write_keys, read_queries, decay_codes, scan_order, masked, skip_gain
):
    space_size = lax.axis_size("space")
    seq_size = lax.axis_size("seq")
    state = write_keys.shape[0]
    tok = features.shape[1]
    length = tok * space_size
    blocks = length // BLOCK
    unit = 0.065536 / (length * seq_size)
    width = features.shape[0] // space_size
    seq_place = lax.axis_index("seq")
    first_token = (seq_place * space_size + lax.axis_index("space")) * tok

    def swap(a, axis):
        return lax.all_to_all(a, axis, split_axis=0, concat_axis=0, tiled=True)

    packet = call(
        packet_kernel, [struct((2, tok, state), bf16)], [], [write_keys[None], read_queries[None]], [], 0, "packet"
    )[0]
    gathered = lax.all_gather(packet, "space", axis=0, tiled=False)
    head_x = swap(features.reshape(space_size, width, tok), "space")
    slot_grid = lax.broadcasted_iota(jnp.int32, (masked.shape[0], tok), 1)
    is_masked = jnp.any((masked - first_token)[:, None] == slot_grid, axis=0)
    marked = jnp.where(is_masked[None], targets, jnp.asarray(MARK, bf16))
    head_t = swap(marked.reshape(space_size, width, tok), "space")
    codes = decay_codes.astype(f32).reshape(length // 128, 1, 128)
    where = seq_place.reshape(1).astype(jnp.int32)
    order = scan_order.reshape(blocks, BLOCK // 128, 128)

    by_block = struct((blocks, BLOCK, state), bf16)
    wide = struct((blocks, BLOCK, 128), f32)
    by_block_t = struct((blocks, state, BLOCK), bf16)
    states = struct((blocks, state, 128), f32)
    payload = struct((1, state + 8, 128), f32)
    heads = struct((space_size, width, tok), bf16)
    small = pltpu.VMEM((BLOCK // 8, 8, 128), f32)
    full = pltpu.VMEM((length, 128), f32)
    read_states = pltpu.VMEM((blocks, state, 256), f32)

    e, total = call(
        partial(decay_kernel, unit),
        [wide, struct((1, 8, 128), f32)],
        [],
        [codes],
        [full, pltpu.VMEM((BLOCK, BLOCK), bf16), small, small],
        2 * 10**9,
        "decay",
        order,
    )
    xt = call(rows_kernel, [by_block], [], [head_x, head_t], [full, small, small], 10**9, "rows", order)[0]
    w, w_t, p, pay = call(
        states_kernel,
        [by_block, by_block_t, states, payload],
        [],
        [gathered, xt, e, total],
        [full, small, small],
        2 * 10**9,
        "states",
        order,
    )
    others = swap(jnp.broadcast_to(pay, (seq_size,) + pay.shape[1:]), "seq")
    q, q_t, near = call(
        near_kernel,
        [by_block, by_block_t, wide],
        [],
        [gathered, xt, e, w_t],
        [full, small, small],
        4 * 10**9,
        "near",
        order,
    )
    y, residue, p, pay = call(
        partial(turn_kernel, unit),
        [by_block, by_block, states, payload],
        [where, skip_gain],
        [q, q_t, xt, e, near, p, total, others],
        [read_states],
        2 * 10**9,
        "turn",
    )
    others = swap(jnp.broadcast_to(pay, (seq_size,) + pay.shape[1:]), "seq")
    mixed_heads, near = call(
        place_kernel,
        [heads, wide],
        [],
        [y, residue, e, w, q_t],
        [full, small, small],
        4 * 10**9,
        "place",
        order,
    )
    mixed = swap(mixed_heads, "space").reshape(features.shape)
    grads_heads = call(
        partial(finish_kernel, unit),
        [heads],
        [where, skip_gain],
        [w, residue, e, near, p, others],
        [read_states, full, small, small],
        2 * 10**9,
        "finish",
        order,
    )[0]
    grad_features = swap(grads_heads, "space").reshape(features.shape)
    return (mixed, grad_features)


def solution(mesh):
    return jax.shard_map(
        per_device,
        mesh=mesh,
        in_specs=(
            P(None, ("seq", "space")),
            P(None, ("seq", "space")),
            P(None, ("seq", "space")),
            P(None, ("seq", "space")),
            P("space", "seq"),
            P(),
            P(("seq", "space")),
            P("space"),
        ),
        out_specs=(P(None, ("seq", "space")), P(None, ("seq", "space"))),
        check_vma=False,
    )
```

```python
from functools import partial

import jax
import jax.numpy as jnp
from jax import lax
from jax.experimental import pallas as pl
from jax.experimental.pallas import tpu as pltpu
from jax.sharding import PartitionSpec as P

BLOCK = 512
MARK = 16384.0
f32, bf16 = jnp.float32, jnp.bfloat16
anywhere = pl.BlockSpec(memory_space=pl.ANY)
smem = pl.BlockSpec(memory_space=pltpu.SMEM)


def call(kernel, outs, scalars, arrays, scratch, flops, name, order=None):
    ordered = order is not None
    args = [*scalars, *([order] if ordered else []), *arrays]
    moved = sum(a.size * a.dtype.itemsize for a in args)
    moved += sum(o.size * o.dtype.itemsize for o in outs)
    held = [pltpu.VMEM(v.shape, v.dtype) for v in [*arrays, *outs]]
    most = max(v.shape[0] for v in [*arrays, *outs])
    sems = pltpu.SemaphoreType.DMA((len(held), most))
    return pl.pallas_call(
        partial(streaming, kernel, len(scalars), ordered, len(arrays), len(outs)),
        out_shape=outs,
        in_specs=[smem] * len(scalars) + [anywhere] * (ordered + len(arrays)),
        out_specs=[anywhere] * len(outs),
        scratch_shapes=[*(order_scratch(order) if ordered else []), *held, sems, *scratch],
        cost_estimate=pl.CostEstimate(flops=flops, bytes_accessed=moved, transcendentals=0),
        name=name,
    )(*args)


class Stream:
    def __init__(self, far, near, sems):
        self.far, self.near, self.sems = far, near, sems
        self.count, self.shape = near.shape[0], near.shape

    def each(self, act):
        lax.fori_loop(0, self.count, lambda i, _: (act(i), 0)[1], 0)

    def inward(self, i):
        return pltpu.make_async_copy(self.far.at[i], self.near.at[i], self.sems.at[i])

    def outward(self, i):
        return pltpu.make_async_copy(self.near.at[i], self.far.at[i], self.sems.at[i])

    def __getitem__(self, i):
        return self.near[i]

    def take(self, i):
        self.inward(i).wait()
        return self.near[i]

    def put(self, i, value):
        self.near[i] = value

    def give(self, i, value):
        self.near[i] = value
        self.outward(i).start()


def order_scratch(order):
    return [pltpu.SMEM(order.shape[1:], jnp.int32)] * 2 + [pltpu.SemaphoreType.DMA((2,))]


class Order:
    def __init__(self, far, near, sems):
        self.far, self.near, self.sems = far, near, sems
        self.last = far.shape[0] - 1

    def copy(self, b, k):
        return pltpu.make_async_copy(self.far.at[jnp.minimum(b, self.last)], self.near[k], self.sems.at[k])

    def row(self, k, i):
        return self.near[k][i // 128, i % 128]


def streaming(kernel, n_scalars, ordered, n_in, n_out, *refs):
    scalars, refs = list(refs[:n_scalars]), refs[n_scalars:]
    n = ordered + n_in + n_out
    far, refs = refs[:n], refs[n:]
    if ordered:
        order = Order(far[0], refs[:2], refs[2])
        far, refs = far[1:], refs[3:]
        order.copy(0, 0).start()
        order.copy(1, 1).start()
        scalars = [order, *scalars]
    n -= ordered
    near, sems, scratch = refs[:n], refs[n], refs[n + 1 :]
    streams = [Stream(f, v, sems.at[k]) for k, (f, v) in enumerate(zip(far, near))]
    for stream in streams[:n_in]:
        stream.each(lambda i, s=stream: s.inward(i).start())
    kernel(*scalars, *streams, *scratch)
    for stream in streams[n_in:]:
        stream.each(lambda i, s=stream: s.outward(i).wait())


def struct(shape, dtype):
    return jax.ShapeDtypeStruct(shape, dtype)


def left_half(shape):
    return lax.broadcasted_iota(jnp.int32, shape, 1) < shape[1] // 2


def lower_part(shape):
    return lax.broadcasted_iota(jnp.int32, shape, 0) >= lax.broadcasted_iota(jnp.int32, shape, 1)


def split(value):
    high = value.astype(bf16)
    return high, (value - high.astype(f32)).astype(bf16)


def gather_rows(order, k, src, dst):
    for i in range(BLOCK):
        dst[i // 8, pl.ds(i % 8, 1), :] = src[pl.ds(order.row(k, i), 1), :]


def scatter_rows(order, k, src, dst):
    for i in range(BLOCK):
        dst[pl.ds(order.row(k, i), 1), :] = src[i // 8, pl.ds(i % 8, 1), :]


def arrive(ins, first):
    for stream in ins:
        for k in range(2):
            stream.inward(first + k).wait()


def leave(outs, first):
    for stream in outs:
        for k in range(2):
            stream.outward(first + k).start()


def gathered_blocks(order, src, bufs, ins, outs, work, init):
    order.copy(0, 0).wait()
    gather_rows(order, 0, src, bufs[0])
    order.copy(2, 0).start()

    def pair(i, carry):
        b = 2 * i
        arrive(ins, b)
        order.copy(b + 1, 1).wait()
        order.copy(b + 2, 0).wait()
        block = bufs[0][...].reshape(BLOCK, 128)
        gather_rows(order, 1, src, bufs[1])
        carry = work(b, block, carry)
        block = bufs[1][...].reshape(BLOCK, 128)
        gather_rows(order, 0, src, bufs[0])
        carry = work(b + 1, block, carry)
        order.copy(b + 3, 1).start()
        order.copy(b + 4, 0).start()
        leave(outs, b)
        return carry

    carry = lax.fori_loop(0, outs[0].count // 2, pair, init)
    order.copy(0, 0).wait()
    order.copy(0, 1).wait()
    return carry


def scattered_blocks(order, bufs, dst, ins, outs, work):
    def put(k, value):
        bufs[k][...] = value.reshape(BLOCK // 8, 8, 128)

    arrive(ins, 0)
    order.copy(0, 0).wait()
    put(0, work(0))
    scatter_rows(order, 0, bufs[0], dst)
    put(1, work(1))
    order.copy(2, 0).start()
    leave(outs, 0)

    def pair(i, _):
        b = 2 * i
        arrive(ins, b)
        order.copy(b - 1, 1).wait()
        order.copy(b, 0).wait()
        scatter_rows(order, 1, bufs[1], dst)
        put(0, work(b))
        scatter_rows(order, 0, bufs[0], dst)
        put(1, work(b + 1))
        order.copy(b + 1, 1).start()
        order.copy(b + 2, 0).start()
        leave(outs, b)
        return 0

    lax.fori_loop(1, ins[0].count // 2, pair, 0)
    order.copy(0, 1).wait()
    scatter_rows(order, 1, bufs[1], dst)
    order.copy(0, 0).wait()


def packet_kernel(write, read, out):
    for k, side in enumerate((write, read)):
        out.give(k, side.take(0).astype(f32).T.astype(bf16))


def decay_kernel(unit, order, codes, e_out, total_out, code_all, tri, *bufs):
    def load(c, sums):
        row = codes.take(c)
        code_all[pl.ds(pl.multiple_of(c * 128, 128), 128), :] = jnp.broadcast_to(row, (128, 128)).T
        return sums + row

    sums = lax.fori_loop(0, codes.count, load, jnp.zeros((1, 128), f32))
    tri[...] = jnp.where(lower_part((BLOCK, BLOCK)), 1.0, 0.0).astype(bf16)
    total = jnp.sum(sums)
    total_out.give(0, jnp.full((8, 128), total, f32))
    rate = jnp.where(left_half((BLOCK, 128)), unit, -unit)

    def block(b, code, earlier):
        reach = jnp.dot(tri[...], code.astype(bf16), preferred_element_type=f32) + earlier
        e_out.put(b, jnp.exp(rate * (reach - 0.5 * total)))
        return reach[BLOCK - 1 : BLOCK, :]

    gathered_blocks(order, code_all, bufs, [], [e_out], block, jnp.zeros((1, 128), f32))


def rows_kernel(places, xt_in, xt_out, xt_all, rows):
    tok = xt_in.shape[2]

    def load(c, _):
        base = pl.multiple_of(c * tok, tok)
        xt_all[pl.ds(base, tok), :] = xt_in.take(c).astype(f32).T
        return 0

    lax.fori_loop(0, xt_in.count, load, 0)

    def block(b, _):
        def some(j, _):
            row = places.at[b * (BLOCK // 128) + j]
            part = rows.at[pl.ds(j * 16, 16)]
            for i in range(128):
                part[i // 8, pl.ds(i % 8, 1), :] = xt_all[pl.ds(row[i], 1), :]
            return 0

        lax.fori_loop(0, BLOCK // 128, some, 0)
        xt_out.give(b, rows[...].reshape(BLOCK, 128).astype(bf16))
        return 0

    lax.fori_loop(0, xt_out.count, block, 0)


def block_states(scaled, into_t):
    p = jnp.dot(into_t, jnp.concatenate(split(scaled), axis=1), preferred_element_type=f32)
    return p[:, :128] + p[:, 128:]


def lower_sum(scaled, from_side, into_t):
    half = BLOCK // 2
    low = scaled.astype(bf16)
    top = jnp.dot(from_side[:half], into_t[:, :half], preferred_element_type=f32)
    end = jnp.dot(from_side[half:], into_t, preferred_element_type=f32)
    keep = lower_part((half, half))
    top = jnp.where(keep, top, 0.0).astype(bf16)
    end = jnp.concatenate([end[:, :half], jnp.where(keep, end[:, half:], 0.0)], axis=1).astype(bf16)
    top = jnp.dot(top, low[:half], preferred_element_type=f32)
    end = jnp.dot(end, low, preferred_element_type=f32)
    return jnp.concatenate([top, end], axis=0)


def unpack(sides, side, rows_all):
    tok = sides.shape[2]

    def load(c, _):
        rows_all[pl.ds(pl.multiple_of(c * tok, tok), tok), :] = sides.take(c)[side].astype(f32)
        return 0

    lax.fori_loop(0, sides.count, load, 0)


def doubled(xt):
    x = xt.astype(f32)
    return jnp.where(left_half((BLOCK, 128)), x, pltpu.roll(x, 64, 1))


def states_kernel(order, write, xt_in, e_in, total, w_out, wt_out, p_out, pay_out, rows_all, *bufs):
    unpack(write, 0, rows_all)

    def block(b, w, summed):
        w_t = w.T.astype(bf16)
        w_out.put(b, w.astype(bf16))
        wt_out.put(b, w_t)
        p = block_states(doubled(xt_in[b]) * e_in[b], w_t)
        p_out.put(b, p)
        return summed + p

    zero = jnp.zeros((128, 128), f32)
    summed = gathered_blocks(order, rows_all, bufs, [xt_in, e_in], [w_out, wt_out, p_out], block, zero)
    pay = jnp.concatenate([summed, total.take(0)], axis=0)
    for g in range(pay_out.count):
        pay_out.give(g, pay)


def near_kernel(order, read, xt_in, e_in, wt_in, q_out, qt_out, near_out, rows_all, *bufs):
    unpack(read, 1, rows_all)

    def block(b, q, _):
        q_low = q.astype(bf16)
        q_out.put(b, q_low)
        qt_out.put(b, q.T.astype(bf16))
        near_out.put(b, lower_sum(doubled(xt_in[b]) * e_in[b], q_low, wt_in[b]))
        return 0

    gathered_blocks(order, rows_all, bufs, [xt_in, e_in, wt_in], [q_out, qt_out, near_out], block, 0)


def prepare(unit, me, p_in, others_in, fr):
    groups, blocks = others_in.count, p_in.count
    others = [others_in.take(g) for g in range(groups)]
    half = left_half((1, 128))
    centers = []
    before = jnp.zeros((1, 128), f32)
    for g in range(groups):
        size = others[g][128:129, :]
        centers.append(before + 0.5 * size)
        before = before + size
    mine = jnp.zeros((1, 128), f32)
    for g in range(groups):
        mine = mine + jnp.where(me == g, centers[g], 0.0)
    init = jnp.zeros((128, 128), f32)
    for g in range(groups):
        factor = jnp.exp(-unit * jnp.abs(mine - centers[g]))
        ahead = jnp.where(g < me, factor, 0.0)
        behind = jnp.where(g > me, factor, 0.0)
        init = init + others[g][0:128, :] * jnp.where(half, ahead, behind)
    left = left_half((128, 128))

    def forward(b, run):
        fr[b, :, 0:128] = run
        return run + p_in.take(b)

    lax.fori_loop(0, blocks, forward, init)

    def backward(i, run):
        b = blocks - 1 - i
        run = run + p_in[b]
        high, low = split(jnp.where(left, fr[b, :, 0:128], run))
        fr[b, :, 0:128] = high.astype(f32)
        fr[b, :, 128:256] = low.astype(f32)
        return run

    lax.fori_loop(0, blocks, backward, init)


def read_out(from_side, fr, near, e):
    read = jnp.dot(from_side, fr.astype(bf16), preferred_element_type=f32)
    z = read[:, :128] + read[:, 128:]
    z = z + jnp.where(left_half((BLOCK, 128)), near, -near)
    z = z * pltpu.roll(e, 64, 1)
    return z + pltpu.roll(z, 64, 1)


def store_positions(y_all, out):
    tok = out.shape[2]

    def store(c, _):
        base = pl.multiple_of(c * tok, tok)
        out.give(c, y_all[pl.ds(base, tok), :].T[0:64, :].astype(bf16))
        return 0

    lax.fori_loop(0, out.count, store, 0)


def turn_kernel(unit, where, skip, from_in, from_t, xt_in, e_in, near_in, p_in, total, others, y_out, res_out, p_out, pay_out, fr):
    prepare(unit, where[0], p_in, others, fr)
    gain = skip[0]
    left = left_half((BLOCK, 128))

    ins = [from_in, from_t, xt_in, e_in, near_in]

    def block(b, summed):
        e = e_in[b]
        xt = xt_in[b].astype(f32)
        tx = pltpu.roll(xt, 64, 1)
        x = jnp.where(left, xt, tx)
        t = jnp.where(left, tx, xt)
        y = (read_out(from_in[b], fr[b], near_in[b], e) + gain * x).astype(bf16)
        y_out.put(b, y)
        residue = jnp.where(t < 1024.0, y.astype(f32) - t, 0.0).astype(bf16)
        res_out.put(b, residue)
        p = block_states(residue.astype(f32) * e, from_t[b])
        p_out.put(b, p)
        return summed + p

    def pair(i, summed):
        arrive(ins, 2 * i)
        summed = block(2 * i + 1, block(2 * i, summed))
        leave([y_out, res_out, p_out], 2 * i)
        return summed

    summed = lax.fori_loop(0, p_in.count // 2, pair, jnp.zeros((128, 128), f32))
    pay = jnp.concatenate([summed, total.take(0)], axis=0)
    for g in range(pay_out.count):
        pay_out.give(g, pay)


def place_kernel(order, y_in, res_in, e_in, into_in, from_t, out, near_out, y_all, *bufs):
    def block(b):
        near_out.put(b, lower_sum(res_in[b].astype(f32) * e_in[b], into_in[b], from_t[b]))
        return y_in[b].astype(f32)

    scattered_blocks(order, bufs, y_all, [y_in, res_in, e_in, into_in, from_t], [near_out], block)
    store_positions(y_all, out)


def finish_kernel(unit, order, where, skip, into_in, res_in, e_in, near_in, p_in, others, out, fr, y_all, *bufs):
    prepare(unit, where[0], p_in, others, fr)
    gain = skip[0]

    def block(b):
        y = read_out(into_in[b], fr[b], near_in[b], e_in[b])
        return y + gain * res_in[b].astype(f32)

    scattered_blocks(order, bufs, y_all, [into_in, res_in, e_in, near_in], [], block)
    store_positions(y_all, out)


def per_device(
    features, targets, write_keys, read_queries, decay_codes, scan_order, masked, skip_gain
):
    space_size = lax.axis_size("space")
    seq_size = lax.axis_size("seq")
    state = write_keys.shape[0]
    tok = features.shape[1]
    length = tok * space_size
    blocks = length // BLOCK
    unit = 0.065536 / (length * seq_size)
    width = features.shape[0] // space_size
    seq_place = lax.axis_index("seq")
    first_token = (seq_place * space_size + lax.axis_index("space")) * tok

    def swap(a, axis):
        return lax.all_to_all(a, axis, split_axis=0, concat_axis=0, tiled=True)

    packet = call(
        packet_kernel, [struct((2, tok, state), bf16)], [], [write_keys[None], read_queries[None]], [], 0, "packet"
    )[0]
    gathered = lax.all_gather(packet, "space", axis=0, tiled=False)
    slot_grid = lax.broadcasted_iota(jnp.int32, (masked.shape[0], tok), 1)
    is_masked = jnp.any((masked - first_token)[:, None] == slot_grid, axis=0)
    marked = jnp.where(is_masked[None], targets, jnp.asarray(MARK, bf16))
    both = [a.reshape(space_size, width, tok) for a in (features, marked)]
    head_xt = swap(jnp.concatenate(both, axis=1), "space")
    codes = decay_codes.astype(f32).reshape(length // 128, 1, 128)
    where = seq_place.reshape(1).astype(jnp.int32)
    order = scan_order.reshape(blocks, BLOCK // 128, 128)

    by_block = struct((blocks, BLOCK, state), bf16)
    wide = struct((blocks, BLOCK, 128), f32)
    by_block_t = struct((blocks, state, BLOCK), bf16)
    states = struct((blocks, state, 128), f32)
    payload = struct((seq_size, state + 8, 128), f32)
    heads = struct((space_size, width, tok), bf16)
    small = pltpu.VMEM((BLOCK // 8, 8, 128), f32)
    full = pltpu.VMEM((length, 128), f32)
    read_states = pltpu.VMEM((blocks, state, 256), f32)

    e, total = call(
        partial(decay_kernel, unit),
        [wide, struct((1, 8, 128), f32)],
        [],
        [codes],
        [full, pltpu.VMEM((BLOCK, BLOCK), bf16), small, small],
        2 * 10**9,
        "decay",
        order,
    )
    places = scan_order.reshape(length // 128, 128)
    xt = call(rows_kernel, [by_block], [places], [head_xt], [full, small], 10**9, "rows")[0]
    w, w_t, p, pay = call(
        states_kernel,
        [by_block, by_block_t, states, payload],
        [],
        [gathered, xt, e, total],
        [full, small, small],
        2 * 10**9,
        "states",
        order,
    )
    others = swap(pay, "seq")
    q, q_t, near = call(
        near_kernel,
        [by_block, by_block_t, wide],
        [],
        [gathered, xt, e, w_t],
        [full, small, small],
        4 * 10**9,
        "near",
        order,
    )
    y, residue, p, pay = call(
        partial(turn_kernel, unit),
        [by_block, by_block, states, payload],
        [where, skip_gain],
        [q, q_t, xt, e, near, p, total, others],
        [read_states],
        2 * 10**9,
        "turn",
    )
    others = swap(pay, "seq")
    mixed_heads, near = call(
        place_kernel,
        [heads, wide],
        [],
        [y, residue, e, w, q_t],
        [full, small, small],
        4 * 10**9,
        "place",
        order,
    )
    mixed = swap(mixed_heads, "space").reshape(features.shape)
    grads_heads = call(
        partial(finish_kernel, unit),
        [heads],
        [where, skip_gain],
        [w, residue, e, near, p, others],
        [read_states, full, small, small],
        2 * 10**9,
        "finish",
        order,
    )[0]
    grad_features = swap(grads_heads, "space").reshape(features.shape)
    return (mixed, grad_features)


def solution(mesh):
    return jax.shard_map(
        per_device,
        mesh=mesh,
        in_specs=(
            P(None, ("seq", "space")),
            P(None, ("seq", "space")),
            P(None, ("seq", "space")),
            P(None, ("seq", "space")),
            P("space", "seq"),
            P(),
            P(("seq", "space")),
            P("space"),
        ),
        out_specs=(P(None, ("seq", "space")), P(None, ("seq", "space"))),
        check_vma=False,
    )
```

```python
from functools import partial

import jax
import jax.numpy as jnp
from jax import lax
from jax.experimental import pallas as pl
from jax.experimental.pallas import tpu as pltpu
from jax.sharding import PartitionSpec as P

BLOCK = 512
MARK = 16384.0
f32, bf16 = jnp.float32, jnp.bfloat16
anywhere = pl.BlockSpec(memory_space=pl.ANY)
smem = pl.BlockSpec(memory_space=pltpu.SMEM)


def call(kernel, outs, scalars, arrays, scratch, flops, name, order=None):
    ordered = order is not None
    args = [*scalars, *([order] if ordered else []), *arrays]
    moved = sum(a.size * a.dtype.itemsize for a in args)
    moved += sum(o.size * o.dtype.itemsize for o in outs)
    held = [pltpu.VMEM(v.shape, v.dtype) for v in [*arrays, *outs]]
    most = max(v.shape[0] for v in [*arrays, *outs])
    sems = pltpu.SemaphoreType.DMA((len(held), most))
    return pl.pallas_call(
        partial(streaming, kernel, len(scalars), ordered, len(arrays), len(outs)),
        out_shape=outs,
        in_specs=[smem] * len(scalars) + [anywhere] * (ordered + len(arrays)),
        out_specs=[anywhere] * len(outs),
        scratch_shapes=[*(order_scratch(order) if ordered else []), *held, sems, *scratch],
        cost_estimate=pl.CostEstimate(flops=flops, bytes_accessed=moved, transcendentals=0),
        name=name,
    )(*args)


class Stream:
    def __init__(self, far, near, sems):
        self.far, self.near, self.sems = far, near, sems
        self.count, self.shape = near.shape[0], near.shape

    def each(self, act):
        lax.fori_loop(0, self.count, lambda i, _: (act(i), 0)[1], 0)

    def inward(self, i):
        return pltpu.make_async_copy(self.far.at[i], self.near.at[i], self.sems.at[i])

    def outward(self, i):
        return pltpu.make_async_copy(self.near.at[i], self.far.at[i], self.sems.at[i])

    def __getitem__(self, i):
        return self.near[i]

    def take(self, i):
        self.inward(i).wait()
        return self.near[i]

    def put(self, i, value):
        self.near[i] = value

    def give(self, i, value):
        self.near[i] = value
        self.outward(i).start()


def order_scratch(order):
    return [pltpu.SMEM(order.shape[1:], jnp.int32)] * 2 + [pltpu.SemaphoreType.DMA((2,))]


class Order:
    def __init__(self, far, near, sems):
        self.far, self.near, self.sems = far, near, sems
        self.last = far.shape[0] - 1

    def copy(self, b, k):
        return pltpu.make_async_copy(self.far.at[jnp.minimum(b, self.last)], self.near[k], self.sems.at[k])

    def row(self, k, i):
        return self.near[k][i // 128, i % 128]


def streaming(kernel, n_scalars, ordered, n_in, n_out, *refs):
    scalars, refs = list(refs[:n_scalars]), refs[n_scalars:]
    n = ordered + n_in + n_out
    far, refs = refs[:n], refs[n:]
    if ordered:
        order = Order(far[0], refs[:2], refs[2])
        far, refs = far[1:], refs[3:]
        order.copy(0, 0).start()
        order.copy(1, 1).start()
        scalars = [order, *scalars]
    n -= ordered
    near, sems, scratch = refs[:n], refs[n], refs[n + 1 :]
    streams = [Stream(f, v, sems.at[k]) for k, (f, v) in enumerate(zip(far, near))]
    for stream in streams[:n_in]:
        stream.each(lambda i, s=stream: s.inward(i).start())
    kernel(*scalars, *streams, *scratch)
    for stream in streams[n_in:]:
        stream.each(lambda i, s=stream: s.outward(i).wait())


def struct(shape, dtype):
    return jax.ShapeDtypeStruct(shape, dtype)


def left_half(shape):
    return lax.broadcasted_iota(jnp.int32, shape, 1) < shape[1] // 2


def lower_part(shape):
    return lax.broadcasted_iota(jnp.int32, shape, 0) >= lax.broadcasted_iota(jnp.int32, shape, 1)


def split(value):
    high = value.astype(bf16)
    return high, (value - high.astype(f32)).astype(bf16)


def gather_rows(order, k, src, dst):
    for i in range(BLOCK):
        dst[i // 8, pl.ds(i % 8, 1), :] = src[pl.ds(order.row(k, i), 1), :]


def scatter_rows(order, k, src, dst):
    for i in range(BLOCK):
        dst[pl.ds(order.row(k, i), 1), :] = src[i // 8, pl.ds(i % 8, 1), :]


def arrive(ins, first):
    for stream in ins:
        for k in range(2):
            stream.inward(first + k).wait()


def leave(outs, first):
    for stream in outs:
        for k in range(2):
            stream.outward(first + k).start()


def gathered_blocks(order, src, bufs, ins, outs, work, init):
    order.copy(0, 0).wait()
    gather_rows(order, 0, src, bufs[0])
    order.copy(2, 0).start()

    def pair(i, carry):
        b = 2 * i
        arrive(ins, b)
        order.copy(b + 1, 1).wait()
        order.copy(b + 2, 0).wait()
        block = bufs[0][...].reshape(BLOCK, 128)
        gather_rows(order, 1, src, bufs[1])
        carry = work(b, block, carry)
        block = bufs[1][...].reshape(BLOCK, 128)
        gather_rows(order, 0, src, bufs[0])
        carry = work(b + 1, block, carry)
        order.copy(b + 3, 1).start()
        order.copy(b + 4, 0).start()
        leave(outs, b)
        return carry

    carry = lax.fori_loop(0, outs[0].count // 2, pair, init)
    order.copy(0, 0).wait()
    order.copy(0, 1).wait()
    return carry


def scattered_blocks(order, bufs, dst, ins, outs, work):
    def put(k, value):
        bufs[k][...] = value.reshape(BLOCK // 8, 8, 128)

    arrive(ins, 0)
    order.copy(0, 0).wait()
    put(0, work(0))
    scatter_rows(order, 0, bufs[0], dst)
    put(1, work(1))
    order.copy(2, 0).start()
    leave(outs, 0)

    def pair(i, _):
        b = 2 * i
        arrive(ins, b)
        order.copy(b - 1, 1).wait()
        order.copy(b, 0).wait()
        scatter_rows(order, 1, bufs[1], dst)
        put(0, work(b))
        scatter_rows(order, 0, bufs[0], dst)
        put(1, work(b + 1))
        order.copy(b + 1, 1).start()
        order.copy(b + 2, 0).start()
        leave(outs, b)
        return 0

    lax.fori_loop(1, ins[0].count // 2, pair, 0)
    order.copy(0, 1).wait()
    scatter_rows(order, 1, bufs[1], dst)
    order.copy(0, 0).wait()


def packet_kernel(write, read, out):
    for k, side in enumerate((write, read)):
        out.give(k, side.take(0).astype(f32).T.astype(bf16))


def decay_kernel(unit, order, codes, e_out, total_out, code_all, tri, *bufs):
    def load(c, sums):
        row = codes.take(c)
        code_all[pl.ds(pl.multiple_of(c * 128, 128), 128), :] = jnp.broadcast_to(row, (128, 128)).T
        return sums + row

    sums = lax.fori_loop(0, codes.count, load, jnp.zeros((1, 128), f32))
    tri[...] = jnp.where(lower_part((BLOCK, BLOCK)), 1.0, 0.0).astype(bf16)
    total = jnp.sum(sums)
    total_out.give(0, jnp.full((8, 128), total, f32))
    rate = jnp.where(left_half((BLOCK, 128)), unit, -unit)

    def block(b, code, earlier):
        reach = jnp.dot(tri[...], code.astype(bf16), preferred_element_type=f32) + earlier
        e_out.put(b, jnp.exp(rate * (reach - 0.5 * total)))
        return reach[BLOCK - 1 : BLOCK, :]

    gathered_blocks(order, code_all, bufs, [], [e_out], block, jnp.zeros((1, 128), f32))


def rows_kernel(places, xt_in, e_in, xt_out, terms_out, xt_all, rows):
    tok = xt_in.shape[2]

    def load(c, _):
        base = pl.multiple_of(c * tok, tok)
        xt_all[pl.ds(base, tok), :] = xt_in.take(c).astype(f32).T
        return 0

    lax.fori_loop(0, xt_in.count, load, 0)

    def block(b, _):
        def some(j, _):
            row = places.at[b * (BLOCK // 128) + j]
            part = rows.at[pl.ds(j * 16, 16)]
            for i in range(128):
                part[i // 8, pl.ds(i % 8, 1), :] = xt_all[pl.ds(row[i], 1), :]
            return 0

        lax.fori_loop(0, BLOCK // 128, some, 0)
        xt = rows[...].reshape(BLOCK, 128)
        xt_out.give(b, xt.astype(bf16))
        both = jnp.where(left_half((BLOCK, 128)), xt, pltpu.roll(xt, 64, 1))
        terms_out.give(b, jnp.concatenate(split(both * e_in.take(b)), axis=1))
        return 0

    lax.fori_loop(0, xt_out.count, block, 0)


def block_states(terms, into_t):
    p = jnp.dot(into_t, terms, preferred_element_type=f32)
    return p[:, :128] + p[:, 128:]


def lower_sum(low, from_side, into_t):
    half = BLOCK // 2
    top = jnp.dot(from_side[:half], into_t[:, :half], preferred_element_type=f32)
    end = jnp.dot(from_side[half:], into_t, preferred_element_type=f32)
    keep = lower_part((half, half))
    top = jnp.where(keep, top, 0.0).astype(bf16)
    end = jnp.concatenate([end[:, :half], jnp.where(keep, end[:, half:], 0.0)], axis=1).astype(bf16)
    top = jnp.dot(top, low[:half], preferred_element_type=f32)
    end = jnp.dot(end, low, preferred_element_type=f32)
    return jnp.concatenate([top, end], axis=0)


def unpack(sides, side, rows_all):
    tok = sides.shape[2]

    def load(c, _):
        rows_all[pl.ds(pl.multiple_of(c * tok, tok), tok), :] = sides.take(c)[side].astype(f32)
        return 0

    lax.fori_loop(0, sides.count, load, 0)


def states_kernel(order, write, terms_in, total, w_out, wt_out, p_out, pay_out, rows_all, *bufs):
    unpack(write, 0, rows_all)

    def block(b, w, summed):
        w_t = w.T.astype(bf16)
        w_out.put(b, w.astype(bf16))
        wt_out.put(b, w_t)
        p = block_states(terms_in[b], w_t)
        p_out.put(b, p)
        return summed + p

    zero = jnp.zeros((128, 128), f32)
    summed = gathered_blocks(order, rows_all, bufs, [terms_in], [w_out, wt_out, p_out], block, zero)
    pay = jnp.concatenate([summed, total.take(0)], axis=0)
    for g in range(pay_out.count):
        pay_out.give(g, pay)


def near_kernel(order, read, terms_in, wt_in, q_out, qt_out, near_out, rows_all, *bufs):
    unpack(read, 1, rows_all)

    def block(b, q, _):
        q_low = q.astype(bf16)
        q_out.put(b, q_low)
        qt_out.put(b, q.T.astype(bf16))
        near_out.put(b, lower_sum(terms_in[b][:, :128], q_low, wt_in[b]))
        return 0

    gathered_blocks(order, rows_all, bufs, [terms_in, wt_in], [q_out, qt_out, near_out], block, 0)


def prepare(unit, me, p_in, others_in, fr):
    groups, blocks = others_in.count, p_in.count
    others = [others_in.take(g) for g in range(groups)]
    half = left_half((1, 128))
    centers = []
    before = jnp.zeros((1, 128), f32)
    for g in range(groups):
        size = others[g][128:129, :]
        centers.append(before + 0.5 * size)
        before = before + size
    mine = jnp.zeros((1, 128), f32)
    for g in range(groups):
        mine = mine + jnp.where(me == g, centers[g], 0.0)
    init = jnp.zeros((128, 128), f32)
    for g in range(groups):
        factor = jnp.exp(-unit * jnp.abs(mine - centers[g]))
        ahead = jnp.where(g < me, factor, 0.0)
        behind = jnp.where(g > me, factor, 0.0)
        init = init + others[g][0:128, :] * jnp.where(half, ahead, behind)
    left = left_half((128, 128))

    def forward(b, run):
        fr[b, :, 0:128] = run
        return run + p_in.take(b)

    lax.fori_loop(0, blocks, forward, init)

    def backward(i, run):
        b = blocks - 1 - i
        run = run + p_in[b]
        high, low = split(jnp.where(left, fr[b, :, 0:128], run))
        fr[b, :, 0:128] = high.astype(f32)
        fr[b, :, 128:256] = low.astype(f32)
        return run

    lax.fori_loop(0, blocks, backward, init)


def read_out(from_side, fr, near, e):
    read = jnp.dot(from_side, fr.astype(bf16), preferred_element_type=f32)
    z = read[:, :128] + read[:, 128:]
    z = z + jnp.where(left_half((BLOCK, 128)), near, -near)
    z = z * pltpu.roll(e, 64, 1)
    return z + pltpu.roll(z, 64, 1)


def store_positions(y_all, out):
    tok = out.shape[2]

    def store(c, _):
        base = pl.multiple_of(c * tok, tok)
        out.give(c, y_all[pl.ds(base, tok), :].T[0:64, :].astype(bf16))
        return 0

    lax.fori_loop(0, out.count, store, 0)


def turn_kernel(unit, where, skip, from_in, from_t, xt_in, e_in, near_in, p_in, total, others, y_out, res_out, p_out, pay_out, fr):
    prepare(unit, where[0], p_in, others, fr)
    gain = skip[0]
    left = left_half((BLOCK, 128))

    ins = [from_in, from_t, xt_in, e_in, near_in]

    def block(b, summed):
        e = e_in[b]
        xt = xt_in[b].astype(f32)
        tx = pltpu.roll(xt, 64, 1)
        x = jnp.where(left, xt, tx)
        t = jnp.where(left, tx, xt)
        y = (read_out(from_in[b], fr[b], near_in[b], e) + gain * x).astype(bf16)
        y_out.put(b, y)
        residue = jnp.where(t < 1024.0, y.astype(f32) - t, 0.0).astype(bf16)
        res_out.put(b, residue)
        p = block_states(jnp.concatenate(split(residue.astype(f32) * e), axis=1), from_t[b])
        p_out.put(b, p)
        return summed + p

    def pair(i, summed):
        arrive(ins, 2 * i)
        summed = block(2 * i + 1, block(2 * i, summed))
        leave([y_out, res_out, p_out], 2 * i)
        return summed

    summed = lax.fori_loop(0, p_in.count // 2, pair, jnp.zeros((128, 128), f32))
    pay = jnp.concatenate([summed, total.take(0)], axis=0)
    for g in range(pay_out.count):
        pay_out.give(g, pay)


def place_kernel(order, y_in, res_in, e_in, into_in, from_t, out, near_out, y_all, *bufs):
    def block(b):
        near_out.put(b, lower_sum((res_in[b].astype(f32) * e_in[b]).astype(bf16), into_in[b], from_t[b]))
        return y_in[b].astype(f32)

    scattered_blocks(order, bufs, y_all, [y_in, res_in, e_in, into_in, from_t], [near_out], block)
    store_positions(y_all, out)


def finish_kernel(unit, order, where, skip, into_in, res_in, e_in, near_in, p_in, others, out, fr, y_all, *bufs):
    prepare(unit, where[0], p_in, others, fr)
    gain = skip[0]

    def block(b):
        y = read_out(into_in[b], fr[b], near_in[b], e_in[b])
        return y + gain * res_in[b].astype(f32)

    scattered_blocks(order, bufs, y_all, [into_in, res_in, e_in, near_in], [], block)
    store_positions(y_all, out)


def per_device(
    features, targets, write_keys, read_queries, decay_codes, scan_order, masked, skip_gain
):
    space_size = lax.axis_size("space")
    seq_size = lax.axis_size("seq")
    state = write_keys.shape[0]
    tok = features.shape[1]
    length = tok * space_size
    blocks = length // BLOCK
    unit = 0.065536 / (length * seq_size)
    width = features.shape[0] // space_size
    seq_place = lax.axis_index("seq")
    first_token = (seq_place * space_size + lax.axis_index("space")) * tok

    def swap(a, axis):
        return lax.all_to_all(a, axis, split_axis=0, concat_axis=0, tiled=True)

    packet = call(
        packet_kernel, [struct((2, tok, state), bf16)], [], [write_keys[None], read_queries[None]], [], 0, "packet"
    )[0]
    gathered = lax.all_gather(packet, "space", axis=0, tiled=False)
    slot_grid = lax.broadcasted_iota(jnp.int32, (masked.shape[0], tok), 1)
    is_masked = jnp.any((masked - first_token)[:, None] == slot_grid, axis=0)
    marked = jnp.where(is_masked[None], targets, jnp.asarray(MARK, bf16))
    both = [a.reshape(space_size, width, tok) for a in (features, marked)]
    head_xt = swap(jnp.concatenate(both, axis=1), "space")
    codes = decay_codes.astype(f32).reshape(length // 128, 1, 128)
    where = seq_place.reshape(1).astype(jnp.int32)
    order = scan_order.reshape(blocks, BLOCK // 128, 128)

    by_block = struct((blocks, BLOCK, state), bf16)
    wide = struct((blocks, BLOCK, 128), f32)
    by_block_t = struct((blocks, state, BLOCK), bf16)
    states = struct((blocks, state, 128), f32)
    payload = struct((seq_size, state + 8, 128), f32)
    heads = struct((space_size, width, tok), bf16)
    small = pltpu.VMEM((BLOCK // 8, 8, 128), f32)
    full = pltpu.VMEM((length, 128), f32)
    read_states = pltpu.VMEM((blocks, state, 256), f32)

    e, total = call(
        partial(decay_kernel, unit),
        [wide, struct((1, 8, 128), f32)],
        [],
        [codes],
        [full, pltpu.VMEM((BLOCK, BLOCK), bf16), small, small],
        2 * 10**9,
        "decay",
        order,
    )
    places = scan_order.reshape(length // 128, 128)
    by_block_terms = struct((blocks, BLOCK, 256), bf16)
    xt, terms = call(
        rows_kernel, [by_block, by_block_terms], [places], [head_xt, e], [full, small], 10**9, "rows"
    )
    w, w_t, p, pay = call(
        states_kernel,
        [by_block, by_block_t, states, payload],
        [],
        [gathered, terms, total],
        [full, small, small],
        2 * 10**9,
        "states",
        order,
    )
    others = swap(pay, "seq")
    q, q_t, near = call(
        near_kernel,
        [by_block, by_block_t, wide],
        [],
        [gathered, terms, w_t],
        [full, small, small],
        4 * 10**9,
        "near",
        order,
    )
    y, residue, p, pay = call(
        partial(turn_kernel, unit),
        [by_block, by_block, states, payload],
        [where, skip_gain],
        [q, q_t, xt, e, near, p, total, others],
        [read_states],
        2 * 10**9,
        "turn",
    )
    others = swap(pay, "seq")
    mixed_heads, near = call(
        place_kernel,
        [heads, wide],
        [],
        [y, residue, e, w, q_t],
        [full, small, small],
        4 * 10**9,
        "place",
        order,
    )
    mixed = swap(mixed_heads, "space").reshape(features.shape)
    grads_heads = call(
        partial(finish_kernel, unit),
        [heads],
        [where, skip_gain],
        [w, residue, e, near, p, others],
        [read_states, full, small, small],
        2 * 10**9,
        "finish",
        order,
    )[0]
    grad_features = swap(grads_heads, "space").reshape(features.shape)
    return (mixed, grad_features)


def solution(mesh):
    return jax.shard_map(
        per_device,
        mesh=mesh,
        in_specs=(
            P(None, ("seq", "space")),
            P(None, ("seq", "space")),
            P(None, ("seq", "space")),
            P(None, ("seq", "space")),
            P("space", "seq"),
            P(),
            P(("seq", "space")),
            P("space"),
        ),
        out_specs=(P(None, ("seq", "space")), P(None, ("seq", "space"))),
        check_vma=False,
    )
```
